256 devices in a mesh: sec: 4 (over x_lo, core), dom: 64 (over y, x_hi, z).
Axes of the slice: x: 4 (x_hi: 2, x_lo: 2; x = x_hi * 2 + x_lo), y: 4, z: 8, core: 2. Of those that a mesh axis runs over, the one named last changes fastest.
Arguments:
- state: float32 [4, 64, 393216], P('sec', None, 'dom'), may hold values from -6 to 6
- send_list: int32 [4, 64, 2, 12], P('sec', 'dom'), may hold values from 0 to 47
- op_index: int32 [4, 3072, 3], P('sec', 'dom'), may hold values from 0 to 71, as said below
- op_weight: float32 [4, 3072, 3, 128, 128], P('sec', 'dom'), may hold values from -0.3125 to 0.3125
- vertical: float32 [4, 64, 64], P('sec'), may hold values from -0.75 to 0.75
- flux_weight: float32 [4, 16, 16], P('sec'), may hold values from -1.5 to 1.5
- remap_index: int32 [3072, 2], P('dom'), may hold values from 0 to 215, as said below
- remap_weight: float32 [3072, 2, 128, 128], P('dom'), may hold values from -0.375 to 0.375
- wet_mask: int32 [393216], P('dom'), may hold values 0 or 1
Outputs:
- state_out: float32 [4, 64, 393216], P('sec', None, 'dom')
The draws below stay inside these ranges and needn't reach their ends.
Inputs may be any that keep to these rules, and one draw needn't show every extreme that they name: `op_index`: indices into a partition's block list E: its 48 own blocks, then 12 from the previous partition, then 12 from the next. `remap_index`: indices into an ocean partition's candidate list of 216 flux blocks.
All inputs are finite; a program needn't handle non-finite values. No bound on the sum of `wet_mask` on one device may be relied on, other than what follows from the above.
Results may differ from the reference program's by a relative error of at most 0.0001.
Values sent between devices are 32-bit elements; how exact they have to be, the bound alone decides.
A program may use at most 128 MiB of HBM per device.

```python
import jax
import jax.numpy as jnp
from jax import lax

NB = 48
B = 128
L = 64
K = 3
R = 2
NFLUX = 16
STEPS = 2
SECS = 4
DOMS = 64
H = 12
SLOTS = 6144
ATM_COLS = 3072
NBA = 24
NSUR = 8


def draw_op_index(key, part):
    first_key, second_key = jax.random.split(key)
    rows = jnp.arange(DOMS * NB, dtype=jnp.int32) % NB
    rows = jnp.broadcast_to(rows[None, :], (SECS, DOMS * NB))
    offset = jax.random.randint(first_key, (SECS, DOMS), 0, 2 * H, dtype=jnp.int32)
    offset = jnp.repeat(offset, NB, axis=1)
    own_entry = rows
    edge_entry = NB + (rows + offset) % (2 * H)
    other_entry = jax.random.randint(second_key, (SECS, DOMS * NB), 0, NB + 2 * H, dtype=jnp.int32)
    return jnp.stack([own_entry, edge_entry, other_entry], axis=2).astype(jnp.int32)


def draw_remap_index(key, part):
    first_key, second_key = jax.random.split(key)
    rows = jnp.arange(DOMS * NB, dtype=jnp.int32) % NB
    within = jax.random.randint(first_key, (DOMS * NB,), 0, NBA, dtype=jnp.int32)
    near_entry = rows % 9 * NBA + within
    other_entry = jax.random.randint(second_key, (DOMS * NB,), 0, 9 * NBA, dtype=jnp.int32)
    return jnp.stack([near_entry, other_entry], axis=1).astype(jnp.int32)


def set_ends(values, own_key, low, largest):
    place = [jax.random.randint(jax.random.fold_in(own_key, axis), (), 0, length) for axis, length in enumerate(values.shape)]
    main_axis = values.shape.index(max(values.shape))
    neighbour = place[:main_axis] + [(place[main_axis] + 1) % values.shape[main_axis]] + place[main_axis + 1:]
    return values.at[tuple(place)].set(low).at[tuple(neighbour)].set(largest)


def level_of(rng, shape, cuts, low, high):
    factor_of = 1.0
    for position, blocks in cuts:
        draws = jax.random.uniform(jax.random.fold_in(jax.random.fold_in(rng, 6), position), (blocks,), jnp.float32, low / len(cuts), high / len(cuts))
        factor_of = factor_of * jnp.repeat(jnp.exp(draws), shape[position] // blocks).reshape((-1,) + (1,) * (len(shape) - 1 - position))
    return factor_of


def bell_draw(rng, dims, scale, bound, shards=(), kind=jnp.bfloat16):
    array = scale * jax.random.normal(rng, dims, jnp.float32)
    if shards:
        array = array * level_of(rng, dims, shards, -0.22, 0.18)
    return jnp.clip(array, -bound, bound).astype(kind)


def setup_inputs(seed: int = 0) -> dict:
    streams_of = jax.random.split(jax.random.key(seed), 10)
    state = bell_draw(streams_of[0], (SECS, L, DOMS * SLOTS), 1.0, 6.0, ((0, 4), (2, 64)), jnp.float32)
    send_list = set_ends(jax.random.randint(streams_of[1], (SECS, DOMS, 2, H), 0, NB), jax.random.fold_in(streams_of[1], 1), 0, NB - 1).astype(jnp.int32)
    op_index = draw_op_index(jax.random.fold_in(streams_of[9], 71), 0)
    op_weight = bell_draw(streams_of[3], (SECS, DOMS * NB, K, B, B), (K * B) ** -0.5, 0.3125, ((0, 4), (1, 64)), jnp.float32)
    vertical = bell_draw(streams_of[4], (SECS, L, L), L ** -0.5, 0.75, ((0, 4),), jnp.float32)
    flux_weight = bell_draw(streams_of[5], (SECS, NFLUX, NFLUX), NFLUX ** -0.5, 1.5, ((0, 4),), jnp.float32)
    remap_index = draw_remap_index(jax.random.fold_in(streams_of[9], 71), 0)
    remap_weight = bell_draw(streams_of[7], (DOMS * NB, R, B, B), (R * B) ** -0.5, 0.375, ((0, 64),), jnp.float32)
    wet_mask = set_ends((jax.random.randint(streams_of[8], (DOMS * SLOTS,), 0, 10) < 7).astype(jnp.int32), jax.random.fold_in(streams_of[8], 1), 0, 1)
    return dict(state=state, send_list=send_list, op_index=op_index, op_weight=op_weight, vertical=vertical, flux_weight=flux_weight, remap_index=remap_index, remap_weight=remap_weight, wet_mask=wet_mask)


def section_product(section_args):
    extended, pattern, weights = section_args
    picked = jnp.take_along_axis(extended, pattern[:, :, None, None], axis=1)
    picked = picked.reshape(DOMS, NB, K, L, B)
    return jnp.einsum("dnklb,dnkbc->dnlc", picked, weights, precision=lax.Precision.HIGHEST)


def one_step(column_state, send_list, op_index, op_weight, vertical, flux_weight, remap_index, remap_weight, wet_columns):
    blocks = column_state.reshape(SECS, L, DOMS, NB, B).transpose(0, 2, 3, 1, 4)
    sent_blocks = jnp.take_along_axis(blocks, send_list.reshape(SECS, DOMS, 2 * H)[:, :, :, None, None], axis=2)
    from_left = jnp.roll(sent_blocks[:, :, H:], 1, axis=1)
    from_right = jnp.roll(sent_blocks[:, :, :H], -1, axis=1)
    extended = jnp.concatenate([blocks, from_left, from_right], axis=2)
    pattern = op_index.reshape(SECS, DOMS, NB * K)
    weights = op_weight.reshape(SECS, DOMS, NB, K, B, B)
    product = lax.map(section_product, (extended, pattern, weights))
    product = product.transpose(0, 3, 1, 2, 4).reshape(SECS, L, DOMS * SLOTS)
    updated = column_state + product
    mixed_field = jnp.einsum("sij,sjc->sic", vertical, updated, precision=lax.Precision.HIGHEST)
    mixed_parts = mixed_field.reshape(SECS, L, DOMS, SLOTS)
    surface = jnp.concatenate([mixed_parts[:, L - NSUR:, :, :ATM_COLS], mixed_parts[:, L - NSUR:, :, ATM_COLS:]], axis=1)
    surface_flux = jnp.tanh(jnp.einsum("sfg,sgdc->sfdc", flux_weight, surface, precision=lax.Precision.HIGHEST))
    atmosphere = surface_flux[:SECS - 1].transpose(0, 2, 1, 3)
    nearby = jnp.stack([jnp.roll(atmosphere, 1, axis=1), atmosphere, jnp.roll(atmosphere, -1, axis=1)], axis=0)
    nearby = nearby.reshape(3, 3, DOMS, NFLUX, NBA, B).transpose(2, 0, 1, 4, 3, 5).reshape(DOMS, 9 * NBA, NFLUX, B)
    chosen = jnp.take_along_axis(nearby, remap_index.reshape(DOMS, NB * R)[:, :, None, None], axis=1)
    chosen = chosen.reshape(DOMS, NB, R, NFLUX, B)
    forcing = jnp.einsum("dnrfb,dnrbc->fdnc", chosen, remap_weight.reshape(DOMS, NB, R, B, B), precision=lax.Precision.HIGHEST)
    forcing = forcing.reshape(NFLUX, DOMS * SLOTS)
    ocean = wet_columns[None, :] * (mixed_field[SECS - 1] + jnp.pad(forcing, ((0, L - NFLUX), (0, 0))))
    return mixed_field.at[SECS - 1].set(ocean)


def reference(state, send_list, op_index, op_weight, vertical, flux_weight, remap_index, remap_weight, wet_mask):
    wet_columns = wet_mask.astype(jnp.float32)
    column_state = state
    for counter in range(STEPS):
        column_state = one_step(column_state, send_list, op_index, op_weight, vertical, flux_weight, remap_index, remap_weight, wet_columns)
    return column_state
```

```python
import functools

import jax
import jax.numpy as jnp
from jax import lax
from jax.experimental import pallas as pl
from jax.experimental.pallas import tpu as pltpu
from jax.sharding import PartitionSpec as P

MESH = pl.DeviceIdType.MESH
STEPS = 2
WCH = 4


def split(v):
    hi = v.astype(jnp.bfloat16)
    lo = (v - hi.astype(jnp.float32)).astype(jnp.bfloat16)
    return hi, lo


def mm(a, b):
    return jnp.dot(a, b, preferred_element_type=jnp.float32)


def kernel(
    secs,
    doms,
    state,
    send_list,
    op_index,
    op_weight,
    vertical,
    flux_weight,
    remap_index,
    remap_weight,
    wet,
    out,
    x,
    eb,
    wf,
    wb,
    rf,
    rb,
    ys,
    sendbuf,
    land,
    fbuf,
    cand0,
    cand1,
    in_sem,
    w_sem,
    r_sem,
    out_sem,
    hs_sem,
    hr_sem,
    fs_sem,
    fr_sem,
    gs_sem,
    gr_sem,
):
    nb, levels, bs = x.shape[1:]
    nh = land.shape[2]
    kd = wb.shape[1]
    nba = nb // 2
    nf = fbuf.shape[2]
    sur = nf // 2
    natm = secs - 1

    sec = lax.axis_index("sec")
    dom = lax.axis_index("dom")
    nxt = lax.rem(dom + 1, doms)
    prv = lax.rem(dom + doms - 1, doms)
    ocean = natm
    is_ocean = sec == ocean
    cands = (cand0, cand1)

    def state_copy(n):
        cols = pl.ds(pl.multiple_of(n * bs, bs), bs)
        return pltpu.make_async_copy(state.at[0, :, cols], x.at[0, n], in_sem)

    @pl.loop(0, nb)
    def _(n):
        state_copy(n).start()

    wn = nb // WCH
    w_copies = [
        pltpu.make_async_copy(
            op_weight.at[pl.ds(c * wn, wn)], wf.at[pl.ds(c * wn, wn)], w_sem.at[c]
        )
        for c in range(WCH)
    ]
    for c in w_copies:
        c.start()
    r_copy = pltpu.make_async_copy(remap_weight, rf, r_sem)

    @pl.when(is_ocean)
    def _():
        r_copy.start()

    barrier = pltpu.get_barrier_semaphore()

    def greet(s, d):
        pl.semaphore_signal(barrier, inc=1, device_id={"sec": s, "dom": d}, device_id_type=MESH)

    greet(sec, prv)
    greet(sec, nxt)

    @pl.when(is_ocean)
    def _():
        for s in range(natm):
            greet(s, dom)
        pl.semaphore_wait(barrier, 2 + natm)

    @pl.when(jnp.logical_not(is_ocean))
    def _():
        greet(ocean, dom)
        pl.semaphore_wait(barrier, 3)

    def halo(step, to_next):
        src = 1 if to_next else 0
        return pltpu.make_async_remote_copy(
            src_ref=sendbuf.at[step, src],
            dst_ref=land.at[step, 1 - src],
            send_sem=hs_sem.at[step, src],
            recv_sem=hr_sem.at[step, 1 - src],
            device_id={"sec": sec, "dom": nxt if to_next else prv},
            device_id_type=MESH,
        )

    def flux(step, s):
        return pltpu.make_async_remote_copy(
            src_ref=fbuf.at[step],
            dst_ref=cands[step].at[1, s],
            send_sem=fs_sem.at[step],
            recv_sem=fr_sem.at[step, s],
            device_id={"sec": ocean, "dom": dom},
            device_id_type=MESH,
        )

    def forward(step, s, to_next):
        o = 0 if to_next else 2
        return pltpu.make_async_remote_copy(
            src_ref=cands[step].at[1, s],
            dst_ref=cands[step].at[o, s],
            send_sem=gs_sem.at[step, s, o // 2],
            recv_sem=gr_sem.at[step, s, o // 2],
            device_id={"sec": ocean, "dom": nxt if to_next else prv},
            device_id_type=MESH,
        )

    def send_halo(step, cur):
        for to_next in (True, False):
            j = 1 if to_next else 0

            @pl.loop(0, nh)
            def _(h):
                sendbuf[step, j, h] = x[cur, send_list[0, 0, j, h]]

            halo(step, to_next).start()

    def split_own(cur):
        @pl.loop(0, nb // 4)
        def _(i):
            for u in range(4):
                hi, lo = split(x[cur, i * 4 + u])
                eb[i * 4 + u, :levels] = hi
                eb[i * 4 + u, levels:] = lo

    pltpu.make_async_copy(x.at[0], x.at[0], in_sem).wait()

    send_halo(0, 0)
    split_own(0)

    vh, vl = split(vertical[0])
    v3 = jnp.concatenate([vh, vh, vl], axis=1)
    fh, fl = split(flux_weight[0])
    f3 = jnp.concatenate([fh, fh, fl], axis=1)

    for c in range(WCH):
        w_copies[c].wait()

        @pl.loop(c * wn, (c + 1) * wn)
        def _(n):
            hi, lo = split(wf[n])
            wb[n, :, :bs] = hi
            wb[n, :, bs:] = lo

    @pl.when(is_ocean)
    def _():
        r_copy.wait()

        @pl.loop(0, nb)
        def _(n):
            hi, lo = split(rf[n])
            rb[n, :, :bs] = hi
            rb[n, :, bs:] = lo

    def out_copy(buf, n):
        cols = pl.ds(pl.multiple_of(n * bs, bs), bs)
        return pltpu.make_async_copy(x.at[buf, n], out.at[0, :, cols], out_sem)

    for step in range(STEPS):
        cur, new = step, step + 1
        halo(step, True).wait_recv()
        halo(step, False).wait_recv()
        for half in range(2):

            @pl.loop(0, nh // 4)
            def _(i):
                for u in range(4):
                    h = i * 4 + u
                    hi, lo = split(land[step, half, h])
                    eb[nb + half * nh + h, :levels] = hi
                    eb[nb + half * nh + h, levels:] = lo

        @pl.loop(0, nb // 4)
        def _(i):
            for u in range(2):
                parts = []
                for t in range(2):
                    n = i * 4 + u * 2 + t
                    lhs = jnp.concatenate(
                        [eb[op_index[k, 0, n]] for k in range(op_index.shape[0])], axis=1
                    )
                    r = mm(lhs, wb[n])
                    y = x[cur, n] + (r[:levels, :bs] + (r[:levels, bs:] + r[levels:, :bs]))
                    parts.append(split(y))
                hi = jnp.concatenate([parts[0][0], parts[1][0]], axis=1)
                lo = jnp.concatenate([parts[0][1], parts[1][1]], axis=1)
                m = i * 2 + u
                ys[m, :levels] = hi
                ys[m, levels : 2 * levels] = lo
                ys[m, 2 * levels :] = hi

        @pl.loop(0, nb // 8)
        def _(i):
            for u in range(4):
                m = i * 4 + u
                r = mm(v3, ys[m])
                x[new, 2 * m] = r[:, :bs]
                x[new, 2 * m + 1] = r[:, bs:]

        @pl.when(jnp.logical_not(is_ocean))
        def _():
            @pl.loop(0, nba // 4)
            def _(i):
                for u in range(2):
                    b = i * 4 + u * 2
                    p = jnp.concatenate(
                        [
                            jnp.concatenate([x[new, b, levels - sur :], x[new, b + 1, levels - sur :]], axis=1),
                            jnp.concatenate(
                                [x[new, nba + b, levels - sur :], x[new, nba + b + 1, levels - sur :]], axis=1
                            ),
                        ],
                        axis=0,
                    )
                    hi, lo = split(p)
                    f = jnp.tanh(mm(f3, jnp.concatenate([hi, lo, hi], axis=0)))
                    fbuf[step, b] = f[:, :bs]
                    fbuf[step, b + 1] = f[:, bs:]

            flux(step, sec).start()
            if step + 1 < STEPS:
                send_halo(step + 1, new)
            else:

                @pl.loop(0, nb)
                def _(n):
                    out_copy(new, n).start()

        @pl.when(is_ocean)
        def _():
            for s in reversed(range(natm)):
                flux(step, s).wait_recv()
                forward(step, s, True).start()
                forward(step, s, False).start()
            for s in reversed(range(natm)):
                forward(step, s, True).wait_recv()
                forward(step, s, False).wait_recv()
            cflat = cands[step].reshape(3 * natm * nba, nf, bs)

            @pl.loop(0, nb // 2)
            def _(i):
                for u in range(2):
                    n = i * 2 + u
                    c = jnp.concatenate(
                        [cflat[remap_index[j, n]] for j in range(remap_index.shape[0])], axis=1
                    )
                    hi, lo = split(c)
                    r = mm(jnp.concatenate([hi, lo], axis=0), rb[n])
                    g = r[:nf, :bs] + (r[:nf, bs:] + r[nf:, :bs])
                    mask = wet[pl.ds(n, 1), :].astype(jnp.float32)
                    x[new, n, :nf] = mask * (x[new, n, :nf] + g)
                    x[new, n, nf:] = mask * x[new, n, nf:]

            if step + 1 < STEPS:
                send_halo(step + 1, new)
            else:

                @pl.loop(0, nb)
                def _(n):
                    out_copy(new, n).start()

        if step + 1 < STEPS:
            split_own(new)

    for step in range(STEPS):
        halo(step, True).wait_send()
        halo(step, False).wait_send()

        @pl.when(is_ocean)
        def _():
            for s in range(natm):
                forward(step, s, True).wait_send()
                forward(step, s, False).wait_send()

        @pl.when(jnp.logical_not(is_ocean))
        def _():
            flux(step, sec).wait_send()

    pltpu.make_async_copy(x.at[STEPS], x.at[STEPS], out_sem).wait()


def solution(mesh):
    secs, doms = mesh.shape["sec"], mesh.shape["dom"]

    def local(
        state, send_list, op_index, op_weight, vertical, flux_weight, remap_index, remap_weight, wet_mask
    ):
        levels, slots = state.shape[1:]
        nk, bs = op_weight.shape[2:4]
        nb = slots // bs
        nh = send_list.shape[3]
        nr = remap_weight.shape[1]
        nf = flux_weight.shape[1]
        natm = secs - 1
        nba = nb // 2
        f32, bf16 = jnp.float32, jnp.bfloat16
        hbm = pl.BlockSpec(memory_space=pl.ANY)
        smem = pl.BlockSpec(memory_space=pltpu.SMEM)
        vmem = pl.BlockSpec(memory_space=pltpu.VMEM)
        dma = pltpu.SemaphoreType.DMA
        return pl.pallas_call(
            functools.partial(kernel, secs, doms),
            out_shape=jax.ShapeDtypeStruct(state.shape, f32),
            in_specs=[hbm, smem, smem, hbm, vmem, vmem, smem, hbm, vmem],
            out_specs=hbm,
            scratch_shapes=[
                pltpu.VMEM((STEPS + 1, nb, levels, bs), f32),
                pltpu.VMEM((nb + 2 * nh, 2 * levels, bs), bf16),
                pltpu.VMEM((nb, nk * bs, bs), f32),
                pltpu.VMEM((nb, nk * bs, 2 * bs), bf16),
                pltpu.VMEM((nb, nr * bs, bs), f32),
                pltpu.VMEM((nb, nr * bs, 2 * bs), bf16),
                pltpu.VMEM((nb // 2, 3 * levels, 2 * bs), bf16),
                pltpu.VMEM((STEPS, 2, nh, levels, bs), f32),
                pltpu.VMEM((STEPS, 2, nh, levels, bs), f32),
                pltpu.VMEM((STEPS, nba, nf, bs), f32),
                pltpu.VMEM((3, natm, nba, nf, bs), f32),
                pltpu.VMEM((3, natm, nba, nf, bs), f32),
                dma,
                dma((WCH,)),
                dma,
                dma,
                dma((STEPS, 2)),
                dma((STEPS, 2)),
                dma((STEPS,)),
                dma((STEPS, natm)),
                dma((STEPS, natm, 2)),
                dma((STEPS, natm, 2)),
            ],
            compiler_params=pltpu.CompilerParams(
                collective_id=0, has_side_effects=True, vmem_limit_bytes=66 * 1000 * 1000
            ),
        )(
            state,
            send_list,
            op_index.transpose(2, 0, 1),
            op_weight.reshape(nb, nk * bs, bs),
            vertical,
            flux_weight,
            remap_index.T,
            remap_weight.reshape(nb, nr * bs, bs),
            wet_mask.reshape(nb, bs),
        )

    in_specs = (
        P("sec", None, "dom"),
        P("sec", "dom", None, None),
        P("sec", "dom", None),
        P("sec", "dom", None, None, None),
        P("sec", None, None),
        P("sec", None, None),
        P("dom", None),
        P("dom", None, None, None),
        P("dom"),
    )
    return jax.shard_map(
        local, mesh=mesh, in_specs=in_specs, out_specs=P("sec", None, "dom"), check_vma=False
    )
```

```python
import functools

import jax
import jax.numpy as jnp
from jax import lax
from jax.experimental import pallas as pl
from jax.experimental.pallas import tpu as pltpu
from jax.sharding import PartitionSpec as P

MESH = pl.DeviceIdType.MESH
STEPS = 2
WCH = 4
FCH = 2


def split(v):
    hi = v.astype(jnp.bfloat16)
    lo = (v - hi.astype(jnp.float32)).astype(jnp.bfloat16)
    return hi, lo


def mm(a, b):
    return jnp.dot(a, b, preferred_element_type=jnp.float32)


def kernel(
    secs,
    doms,
    state,
    send_list,
    op_index,
    op_weight,
    vertical,
    flux_weight,
    remap_index,
    remap_weight,
    wet,
    out,
    x,
    eb,
    wf,
    wb,
    rf,
    rb,
    ys,
    sendbuf,
    land,
    fbuf,
    relay,
    cand0,
    cand1,
    in_sem,
    w_sem,
    r_sem,
    out_sem,
    hs_sem,
    hr_sem,
    fs_sem,
    fr_sem,
    gs_sem,
    gr_sem,
):
    nb, levels, bs = x.shape[1:]
    nh = land.shape[2]
    kd = wb.shape[1]
    nba = nb // 2
    nf = fbuf.shape[2]
    sur = nf // 2
    natm = secs - 1

    sec = lax.axis_index("sec")
    dom = lax.axis_index("dom")
    nxt = lax.rem(dom + 1, doms)
    prv = lax.rem(dom + doms - 1, doms)
    ocean = natm
    hub = natm - 1
    is_ocean = sec == ocean
    is_hub = sec == hub
    fc = nba // FCH
    around = ((0, nxt), (2, prv), (1, dom))
    rows = (pl.ds(nf, levels - nf), pl.ds(0, nf))
    cands = (cand0, cand1)

    def state_copy(n):
        cols = pl.ds(pl.multiple_of(n * bs, bs), bs)
        return pltpu.make_async_copy(state.at[0, :, cols], x.at[0, n], in_sem)

    @pl.loop(0, nb)
    def _(n):
        state_copy(n).start()

    wn = nb // WCH
    w_copies = [
        pltpu.make_async_copy(
            op_weight.at[pl.ds(c * wn, wn)], wf.at[pl.ds(c * wn, wn)], w_sem.at[c]
        )
        for c in range(WCH)
    ]
    for c in w_copies:
        c.start()
    r_copy = pltpu.make_async_copy(remap_weight, rf, r_sem)

    @pl.when(is_ocean)
    def _():
        r_copy.start()

    barrier = pltpu.get_barrier_semaphore()

    def greet(s, d):
        pl.semaphore_signal(barrier, inc=1, device_id={"sec": s, "dom": d}, device_id_type=MESH)

    greet(sec, prv)
    greet(sec, nxt)

    @pl.when(is_ocean)
    def _():
        for _, d in around:
            greet(hub, d)
        pl.semaphore_wait(barrier, 5)

    @pl.when(is_hub)
    def _():
        for _, d in around:
            greet(ocean, d)
        for s in range(hub):
            greet(s, dom)
        pl.semaphore_wait(barrier, 5 + hub)

    @pl.when(sec < hub)
    def _():
        greet(hub, dom)
        pl.semaphore_wait(barrier, 3)

    def halo(step, to_next, part):
        src = 1 if to_next else 0
        return pltpu.make_async_remote_copy(
            src_ref=sendbuf.at[step, src, :, rows[part]],
            dst_ref=land.at[step, 1 - src, :, rows[part]],
            send_sem=hs_sem.at[step, src, part],
            recv_sem=hr_sem.at[step, 1 - src, part],
            device_id={"sec": sec, "dom": nxt if to_next else prv},
            device_id_type=MESH,
        )

    def flux(step, s, c):
        return pltpu.make_async_remote_copy(
            src_ref=fbuf.at[step, pl.ds(c * fc, fc)],
            dst_ref=relay.at[step, s, pl.ds(c * fc, fc)],
            send_sem=fs_sem.at[step, c],
            recv_sem=fr_sem.at[step, s, c],
            device_id={"sec": hub, "dom": dom},
            device_id_type=MESH,
        )

    def forward(step, s, c, o, d):
        src = fbuf.at[step] if s == hub else relay.at[step, s]
        return pltpu.make_async_remote_copy(
            src_ref=src.at[pl.ds(c * fc, fc)],
            dst_ref=cands[step].at[o, s, pl.ds(c * fc, fc)],
            send_sem=gs_sem.at[step, s, c, o],
            recv_sem=gr_sem.at[step, s, c, o],
            device_id={"sec": ocean, "dom": d},
            device_id_type=MESH,
        )

    def send_halo(step, cur, part):
        for to_next in (True, False):
            j = 1 if to_next else 0

            @pl.loop(0, nh)
            def _(h):
                sendbuf[step, j, h, rows[part]] = x[cur, send_list[0, 0, j, h], rows[part]]

            halo(step, to_next, part).start()

    def put_split(n, v, part):
        start, size = rows[part].start, rows[part].size
        hi, lo = split(v)
        eb[n, pl.ds(start, size)] = hi
        eb[n, pl.ds(levels + start, size)] = lo

    def split_own(cur, part):
        @pl.loop(0, nb // 4)
        def _(i):
            for u in range(4):
                put_split(i * 4 + u, x[cur, i * 4 + u, rows[part]], part)

    def take_halo(step, part):
        halo(step, True, part).wait_recv()
        halo(step, False, part).wait_recv()
        for half in range(2):

            @pl.loop(0, nh // 4)
            def _(i):
                for u in range(4):
                    h = i * 4 + u
                    put_split(nb + half * nh + h, land[step, half, h, rows[part]], part)

    pltpu.make_async_copy(x.at[0], x.at[0], in_sem).wait()

    for part in range(2):
        send_halo(0, 0, part)
    for part in range(2):
        split_own(0, part)

    vh, vl = split(vertical[0])
    v3 = jnp.concatenate([vh, vh, vl], axis=1)
    fh, fl = split(flux_weight[0])
    f3 = jnp.concatenate([fh, fh, fl], axis=1)

    for c in range(WCH):
        w_copies[c].wait()

        @pl.loop(c * wn, (c + 1) * wn)
        def _(n):
            hi, lo = split(wf[n])
            wb[n, :, :bs] = hi
            wb[n, :, bs:] = lo

    @pl.when(is_ocean)
    def _():
        r_copy.wait()

        @pl.loop(0, nb)
        def _(n):
            hi, lo = split(rf[n])
            rb[n, :, :bs] = hi
            rb[n, :, bs:] = lo

    def send_out(part):
        @pl.loop(0, nb)
        def _(n):
            cols = pl.ds(pl.multiple_of(n * bs, bs), bs)
            pltpu.make_async_copy(
                x.at[STEPS, n, rows[part]], out.at[0, rows[part], cols], out_sem
            ).start()

    def step_chunk(cur, new, c):
        hp = nba // 2
        cp = hp // FCH

        def pair(j):
            return j + c * cp + j // cp * (hp - cp)

        @pl.loop(0, cp)
        def _(i):
            for u in range(2):
                m = pair(i * 2 + u)
                parts = []
                for t in range(2):
                    n = m * 2 + t
                    lhs = jnp.concatenate(
                        [eb[op_index[k, 0, n]] for k in range(op_index.shape[0])], axis=1
                    )
                    r = mm(lhs, wb[n])
                    y = x[cur, n] + (r[:levels, :bs] + (r[:levels, bs:] + r[levels:, :bs]))
                    parts.append(split(y))
                hi = jnp.concatenate([parts[0][0], parts[1][0]], axis=1)
                lo = jnp.concatenate([parts[0][1], parts[1][1]], axis=1)
                ys[m, :levels] = hi
                ys[m, levels : 2 * levels] = lo
                ys[m, 2 * levels :] = hi

        @pl.loop(0, cp // 2)
        def _(i):
            for u in range(4):
                m = pair(i * 4 + u)
                r = mm(v3, ys[m])
                x[new, 2 * m] = r[:, :bs]
                x[new, 2 * m + 1] = r[:, bs:]

    for step in range(STEPS):
        cur, new = step, step + 1
        last = new == STEPS
        if step == 0:
            take_halo(step, 0)
            take_halo(step, 1)
        else:

            @pl.when(jnp.logical_not(is_ocean))
            def _():
                take_halo(step, 0)

            take_halo(step, 1)

        for c in range(FCH):
            step_chunk(cur, new, c)

            @pl.when(jnp.logical_not(is_ocean))
            def _():
                @pl.loop(0, fc // 4)
                def _(i):
                    for u in range(2):
                        b = c * fc + i * 4 + u * 2
                        p = jnp.concatenate(
                            [
                                jnp.concatenate([x[new, b, levels - sur :], x[new, b + 1, levels - sur :]], axis=1),
                                jnp.concatenate(
                                    [x[new, nba + b, levels - sur :], x[new, nba + b + 1, levels - sur :]], axis=1
                                ),
                            ],
                            axis=0,
                        )
                        hi, lo = split(p)
                        f = jnp.tanh(mm(f3, jnp.concatenate([hi, lo, hi], axis=0)))
                        fbuf[step, b] = f[:, :bs]
                        fbuf[step, b + 1] = f[:, bs:]

            @pl.when(sec < hub)
            def _():
                flux(step, sec, c).start()

            @pl.when(is_hub)
            def _():
                for o, d in around:
                    forward(step, hub, c, o, d).start()

        @pl.when(is_hub)
        def _():
            for c in range(FCH):
                for s in range(hub):
                    flux(step, s, c).wait_recv()
                    for o, d in around:
                        forward(step, s, c, o, d).start()

        @pl.when(jnp.logical_not(is_ocean))
        def _():
            for part in range(2):
                if last:
                    send_out(part)
                else:
                    send_halo(step + 1, new, part)
            if not last:
                for part in range(2):
                    split_own(new, part)

        @pl.when(is_ocean)
        def _():
            @pl.loop(0, nb // 4)
            def _(i):
                for u in range(4):
                    n = i * 4 + u
                    x[new, n, nf:] = wet[pl.ds(n, 1), :].astype(jnp.float32) * x[new, n, nf:]

            if last:
                send_out(0)
            else:
                send_halo(step + 1, new, 0)
                split_own(new, 0)
                take_halo(step + 1, 0)

            for c in range(FCH):
                for s in range(natm):
                    for o, d in around:
                        forward(step, s, c, o, d).wait_recv()
            cflat = cands[step].reshape(3 * natm * nba, nf, bs)

            @pl.loop(0, nb // 4)
            def _(i):
                for u in range(4):
                    n = i * 4 + u
                    c = jnp.concatenate(
                        [cflat[remap_index[j, n]] for j in range(remap_index.shape[0])], axis=1
                    )
                    hi, lo = split(c)
                    r = mm(jnp.concatenate([hi, lo], axis=0), rb[n])
                    g = r[:nf, :bs] + (r[:nf, bs:] + r[nf:, :bs])
                    mask = wet[pl.ds(n, 1), :].astype(jnp.float32)
                    x[new, n, :nf] = mask * (x[new, n, :nf] + g)

            if last:
                send_out(1)
            else:
                send_halo(step + 1, new, 1)
                split_own(new, 1)

    for step in range(STEPS):
        for part in range(2):
            halo(step, True, part).wait_send()
            halo(step, False, part).wait_send()

        for c in range(FCH):

            @pl.when(is_hub)
            def _():
                for s in range(natm):
                    for o, d in around:
                        forward(step, s, c, o, d).wait_send()

            @pl.when(sec < hub)
            def _():
                flux(step, sec, c).wait_send()

    pltpu.make_async_copy(x.at[STEPS], x.at[STEPS], out_sem).wait()


def solution(mesh):
    secs, doms = mesh.shape["sec"], mesh.shape["dom"]

    def local(
        state, send_list, op_index, op_weight, vertical, flux_weight, remap_index, remap_weight, wet_mask
    ):
        levels, slots = state.shape[1:]
        nk, bs = op_weight.shape[2:4]
        nb = slots // bs
        nh = send_list.shape[3]
        nr = remap_weight.shape[1]
        nf = flux_weight.shape[1]
        natm = secs - 1
        nba = nb // 2
        f32, bf16 = jnp.float32, jnp.bfloat16
        hbm = pl.BlockSpec(memory_space=pl.ANY)
        smem = pl.BlockSpec(memory_space=pltpu.SMEM)
        vmem = pl.BlockSpec(memory_space=pltpu.VMEM)
        dma = pltpu.SemaphoreType.DMA
        return pl.pallas_call(
            functools.partial(kernel, secs, doms),
            out_shape=jax.ShapeDtypeStruct(state.shape, f32),
            in_specs=[hbm, smem, smem, hbm, vmem, vmem, smem, hbm, vmem],
            out_specs=hbm,
            scratch_shapes=[
                pltpu.VMEM((STEPS + 1, nb, levels, bs), f32),
                pltpu.VMEM((nb + 2 * nh, 2 * levels, bs), bf16),
                pltpu.VMEM((nb, nk * bs, bs), f32),
                pltpu.VMEM((nb, nk * bs, 2 * bs), bf16),
                pltpu.VMEM((nb, nr * bs, bs), f32),
                pltpu.VMEM((nb, nr * bs, 2 * bs), bf16),
                pltpu.VMEM((nb // 2, 3 * levels, 2 * bs), bf16),
                pltpu.VMEM((STEPS, 2, nh, levels, bs), f32),
                pltpu.VMEM((STEPS, 2, nh, levels, bs), f32),
                pltpu.VMEM((STEPS, nba, nf, bs), f32),
                pltpu.VMEM((STEPS, natm - 1, nba, nf, bs), f32),
                pltpu.VMEM((3, natm, nba, nf, bs), f32),
                pltpu.VMEM((3, natm, nba, nf, bs), f32),
                dma,
                dma((WCH,)),
                dma,
                dma,
                dma((STEPS, 2, 2)),
                dma((STEPS, 2, 2)),
                dma((STEPS, FCH)),
                dma((STEPS, natm - 1, FCH)),
                dma((STEPS, natm, FCH, 3)),
                dma((STEPS, natm, FCH, 3)),
            ],
            compiler_params=pltpu.CompilerParams(
                collective_id=0, has_side_effects=True, vmem_limit_bytes=66 * 1000 * 1000
            ),
        )(
            state,
            send_list,
            op_index.transpose(2, 0, 1),
            op_weight.reshape(nb, nk * bs, bs),
            vertical,
            flux_weight,
            remap_index.T,
            remap_weight.reshape(nb, nr * bs, bs),
            wet_mask.reshape(nb, bs),
        )

    in_specs = (
        P("sec", None, "dom"),
        P("sec", "dom", None, None),
        P("sec", "dom", None),
        P("sec", "dom", None, None, None),
        P("sec", None, None),
        P("sec", None, None),
        P("dom", None),
        P("dom", None, None, None),
        P("dom"),
    )
    return jax.shard_map(
        local, mesh=mesh, in_specs=in_specs, out_specs=P("sec", None, "dom"), check_vma=False
    )
```

```python
import functools

import jax
import jax.numpy as jnp
from jax import lax
from jax.experimental import pallas as pl
from jax.experimental.pallas import tpu as pltpu
from jax.sharding import PartitionSpec as P

MESH = pl.DeviceIdType.MESH
STEPS = 2
WCH = 4
FCH = 2


def split(v):
    hi = v.astype(jnp.bfloat16)
    lo = (v - hi.astype(jnp.float32)).astype(jnp.bfloat16)
    return hi, lo


def mm(a, b):
    return jnp.dot(a, b, preferred_element_type=jnp.float32)


def kernel(
    secs,
    doms,
    state,
    send_list,
    op_index,
    op_weight,
    vertical,
    flux_weight,
    remap_index,
    remap_weight,
    wet,
    out,
    x,
    eb,
    wf,
    wb,
    rf,
    rb,
    ys,
    sendbuf,
    land,
    fbuf,
    relay,
    cand0,
    cand1,
    in_sem,
    w_sem,
    r_sem,
    out_sem,
    hs_sem,
    hr_sem,
    fs_sem,
    fr_sem,
    gs_sem,
    gr_sem,
):
    nb, levels, bs = x.shape[1:]
    nh = land.shape[2]
    kd = wb.shape[1]
    nba = nb // 2
    nf = fbuf.shape[2]
    sur = nf // 2
    natm = secs - 1

    sec = lax.axis_index("sec")
    dom = lax.axis_index("dom")
    nxt = lax.rem(dom + 1, doms)
    prv = lax.rem(dom + doms - 1, doms)
    ocean = natm
    hub = natm - 1
    is_ocean = sec == ocean
    is_hub = sec == hub
    fc = nba // FCH
    around = ((0, nxt), (2, prv), (1, dom))
    rows = (pl.ds(nf, levels - nf), pl.ds(0, nf))
    cands = (cand0, cand1)

    def state_copy(n):
        cols = pl.ds(pl.multiple_of(n * bs, bs), bs)
        return pltpu.make_async_copy(state.at[0, :, cols], x.at[0, n], in_sem)

    @pl.loop(0, nb)
    def _(n):
        state_copy(n).start()

    wn = nb // WCH
    w_copies = [
        pltpu.make_async_copy(
            op_weight.at[pl.ds(c * wn, wn)], wf.at[pl.ds(c * wn, wn)], w_sem.at[c]
        )
        for c in range(WCH)
    ]
    for c in w_copies:
        c.start()
    r_copy = pltpu.make_async_copy(remap_weight, rf, r_sem)

    @pl.when(is_ocean)
    def _():
        r_copy.start()

    barrier = pltpu.get_barrier_semaphore()

    def greet(s, d):
        pl.semaphore_signal(barrier, inc=1, device_id={"sec": s, "dom": d}, device_id_type=MESH)

    greet(sec, prv)
    greet(sec, nxt)

    @pl.when(is_ocean)
    def _():
        for _, d in around:
            greet(hub, d)
        pl.semaphore_wait(barrier, 5)

    @pl.when(is_hub)
    def _():
        for _, d in around:
            greet(ocean, d)
        for s in range(hub):
            greet(s, dom)
        pl.semaphore_wait(barrier, 5 + hub)

    @pl.when(sec < hub)
    def _():
        greet(hub, dom)
        pl.semaphore_wait(barrier, 3)

    def halo(step, to_next, part):
        src = 1 if to_next else 0
        return pltpu.make_async_remote_copy(
            src_ref=sendbuf.at[step, src, :, rows[part]],
            dst_ref=land.at[step, 1 - src, :, rows[part]],
            send_sem=hs_sem.at[step, src, part],
            recv_sem=hr_sem.at[step, 1 - src, part],
            device_id={"sec": sec, "dom": nxt if to_next else prv},
            device_id_type=MESH,
        )

    def flux(step, s, c):
        return pltpu.make_async_remote_copy(
            src_ref=fbuf.at[step, pl.ds(c * fc, fc)],
            dst_ref=relay.at[step, s, pl.ds(c * fc, fc)],
            send_sem=fs_sem.at[step, c],
            recv_sem=fr_sem.at[step, s, c],
            device_id={"sec": hub, "dom": dom},
            device_id_type=MESH,
        )

    def forward(step, s, c, o, d):
        src = fbuf.at[step] if s == hub else relay.at[step, s]
        return pltpu.make_async_remote_copy(
            src_ref=src.at[pl.ds(c * fc, fc)],
            dst_ref=cands[step].at[o, s, pl.ds(c * fc, fc)],
            send_sem=gs_sem.at[step, s, c, o],
            recv_sem=gr_sem.at[step, s, c, o],
            device_id={"sec": ocean, "dom": d},
            device_id_type=MESH,
        )

    def pass_on(step, c):
        for s in range(hub):
            flux(step, s, c).wait_recv()
            for o, d in around:
                forward(step, s, c, o, d).start()

    def send_halo(step, cur, part):
        for to_next in (True, False):
            j = 1 if to_next else 0

            @pl.loop(0, nh)
            def _(h):
                sendbuf[step, j, h, rows[part]] = x[cur, send_list[0, 0, j, h], rows[part]]

            halo(step, to_next, part).start()

    def put_split(n, v, part):
        start, size = rows[part].start, rows[part].size
        hi, lo = split(v)
        eb[n, pl.ds(start, size)] = hi
        eb[n, pl.ds(levels + start, size)] = lo

    def split_own(cur, part):
        @pl.loop(0, nb // 4)
        def _(i):
            for u in range(4):
                put_split(i * 4 + u, x[cur, i * 4 + u, rows[part]], part)

    def take_halo(step, part):
        halo(step, True, part).wait_recv()
        halo(step, False, part).wait_recv()
        for half in range(2):

            @pl.loop(0, nh // 4)
            def _(i):
                for u in range(4):
                    h = i * 4 + u
                    put_split(nb + half * nh + h, land[step, half, h, rows[part]], part)

    pltpu.make_async_copy(x.at[0], x.at[0], in_sem).wait()

    for part in range(2):
        send_halo(0, 0, part)
    for part in range(2):
        split_own(0, part)

    vh, vl = split(vertical[0])
    v3 = jnp.concatenate([vh, vh, vl], axis=1)
    fh, fl = split(flux_weight[0])
    f3 = jnp.concatenate([fh, fh, fl], axis=1)

    for c in range(WCH):
        w_copies[c].wait()

        @pl.loop(c * wn, (c + 1) * wn)
        def _(n):
            hi, lo = split(wf[n])
            wb[n, :, :bs] = hi
            wb[n, :, bs:] = lo

    @pl.when(is_ocean)
    def _():
        r_copy.wait()

        @pl.loop(0, nb)
        def _(n):
            hi, lo = split(rf[n])
            rb[n, :, :bs] = hi
            rb[n, :, bs:] = lo

    def send_out(part):
        @pl.loop(0, nb)
        def _(n):
            cols = pl.ds(pl.multiple_of(n * bs, bs), bs)
            pltpu.make_async_copy(
                x.at[STEPS, n, rows[part]], out.at[0, rows[part], cols], out_sem
            ).start()

    def step_chunk(cur, new, c):
        hp = nba // 2
        cp = hp // FCH

        def pair(j):
            return j + c * cp + j // cp * (hp - cp)

        @pl.loop(0, cp)
        def _(i):
            for u in range(2):
                m = pair(i * 2 + u)
                parts = []
                for t in range(2):
                    n = m * 2 + t
                    lhs = jnp.concatenate(
                        [eb[op_index[k, 0, n]] for k in range(op_index.shape[0])], axis=1
                    )
                    r = mm(lhs, wb[n])
                    y = x[cur, n] + (r[:levels, :bs] + (r[:levels, bs:] + r[levels:, :bs]))
                    parts.append(split(y))
                hi = jnp.concatenate([parts[0][0], parts[1][0]], axis=1)
                lo = jnp.concatenate([parts[0][1], parts[1][1]], axis=1)
                ys[m, :levels] = hi
                ys[m, levels : 2 * levels] = lo
                ys[m, 2 * levels :] = hi

        @pl.loop(0, cp // 2)
        def _(i):
            for u in range(4):
                m = pair(i * 4 + u)
                r = mm(v3, ys[m])
                x[new, 2 * m] = r[:, :bs]
                x[new, 2 * m + 1] = r[:, bs:]

    for step in range(STEPS):
        cur, new = step, step + 1
        last = new == STEPS
        if step == 0:
            take_halo(step, 0)
            take_halo(step, 1)
        else:

            @pl.when(jnp.logical_not(is_ocean))
            def _():
                take_halo(step, 0)

            take_halo(step, 1)

        for c in range(FCH):
            step_chunk(cur, new, c)

            @pl.when(jnp.logical_not(is_ocean))
            def _():
                @pl.loop(0, fc // 4)
                def _(i):
                    for u in range(2):
                        b = c * fc + i * 4 + u * 2
                        p = jnp.concatenate(
                            [
                                jnp.concatenate([x[new, b, levels - sur :], x[new, b + 1, levels - sur :]], axis=1),
                                jnp.concatenate(
                                    [x[new, nba + b, levels - sur :], x[new, nba + b + 1, levels - sur :]], axis=1
                                ),
                            ],
                            axis=0,
                        )
                        hi, lo = split(p)
                        f = jnp.tanh(mm(f3, jnp.concatenate([hi, lo, hi], axis=0)))
                        fbuf[step, b] = f[:, :bs]
                        fbuf[step, b + 1] = f[:, bs:]

            @pl.when(sec < hub)
            def _():
                flux(step, sec, c).start()

            @pl.when(is_hub)
            def _():
                for o, d in around:
                    forward(step, hub, c, o, d).start()
                if last:
                    pass_on(step, c)
                elif c > 0:
                    pass_on(step, c - 1)

        @pl.when(jnp.logical_not(is_ocean))
        def _():
            for part in range(2):
                if last:
                    send_out(part)
                else:
                    send_halo(step + 1, new, part)
            if not last:

                @pl.when(is_hub)
                def _():
                    pass_on(step, FCH - 1)

                for part in range(2):
                    split_own(new, part)

        @pl.when(is_ocean)
        def _():
            @pl.loop(0, nb // 4)
            def _(i):
                for u in range(4):
                    n = i * 4 + u
                    x[new, n, nf:] = wet[pl.ds(n, 1), :].astype(jnp.float32) * x[new, n, nf:]

            if last:
                send_out(0)
            else:
                send_halo(step + 1, new, 0)
                split_own(new, 0)
                take_halo(step + 1, 0)

            for c in range(FCH):
                for s in range(natm):
                    for o, d in around:
                        forward(step, s, c, o, d).wait_recv()
            cflat = cands[step].reshape(3 * natm * nba, nf, bs)

            @pl.loop(0, nb // 4)
            def _(i):
                for u in range(4):
                    n = i * 4 + u
                    c = jnp.concatenate(
                        [cflat[remap_index[j, n]] for j in range(remap_index.shape[0])], axis=1
                    )
                    hi, lo = split(c)
                    r = mm(jnp.concatenate([hi, lo], axis=0), rb[n])
                    g = r[:nf, :bs] + (r[:nf, bs:] + r[nf:, :bs])
                    mask = wet[pl.ds(n, 1), :].astype(jnp.float32)
                    x[new, n, :nf] = mask * (x[new, n, :nf] + g)

            if last:
                send_out(1)
            else:
                send_halo(step + 1, new, 1)
                split_own(new, 1)

    for step in range(STEPS):
        for part in range(2):
            halo(step, True, part).wait_send()
            halo(step, False, part).wait_send()

        for c in range(FCH):

            @pl.when(is_hub)
            def _():
                for s in range(natm):
                    for o, d in around:
                        forward(step, s, c, o, d).wait_send()

            @pl.when(sec < hub)
            def _():
                flux(step, sec, c).wait_send()

    pltpu.make_async_copy(x.at[STEPS], x.at[STEPS], out_sem).wait()


def solution(mesh):
    secs, doms = mesh.shape["sec"], mesh.shape["dom"]

    def local(
        state, send_list, op_index, op_weight, vertical, flux_weight, remap_index, remap_weight, wet_mask
    ):
        levels, slots = state.shape[1:]
        nk, bs = op_weight.shape[2:4]
        nb = slots // bs
        nh = send_list.shape[3]
        nr = remap_weight.shape[1]
        nf = flux_weight.shape[1]
        natm = secs - 1
        nba = nb // 2
        f32, bf16 = jnp.float32, jnp.bfloat16
        hbm = pl.BlockSpec(memory_space=pl.ANY)
        smem = pl.BlockSpec(memory_space=pltpu.SMEM)
        vmem = pl.BlockSpec(memory_space=pltpu.VMEM)
        dma = pltpu.SemaphoreType.DMA
        return pl.pallas_call(
            functools.partial(kernel, secs, doms),
            out_shape=jax.ShapeDtypeStruct(state.shape, f32),
            in_specs=[hbm, smem, smem, hbm, vmem, vmem, smem, hbm, vmem],
            out_specs=hbm,
            scratch_shapes=[
                pltpu.VMEM((STEPS + 1, nb, levels, bs), f32),
                pltpu.VMEM((nb + 2 * nh, 2 * levels, bs), bf16),
                pltpu.VMEM((nb, nk * bs, bs), f32),
                pltpu.VMEM((nb, nk * bs, 2 * bs), bf16),
                pltpu.VMEM((nb, nr * bs, bs), f32),
                pltpu.VMEM((nb, nr * bs, 2 * bs), bf16),
                pltpu.VMEM((nb // 2, 3 * levels, 2 * bs), bf16),
                pltpu.VMEM((STEPS, 2, nh, levels, bs), f32),
                pltpu.VMEM((STEPS, 2, nh, levels, bs), f32),
                pltpu.VMEM((STEPS, nba, nf, bs), f32),
                pltpu.VMEM((STEPS, natm - 1, nba, nf, bs), f32),
                pltpu.VMEM((3, natm, nba, nf, bs), f32),
                pltpu.VMEM((3, natm, nba, nf, bs), f32),
                dma,
                dma((WCH,)),
                dma,
                dma,
                dma((STEPS, 2, 2)),
                dma((STEPS, 2, 2)),
                dma((STEPS, FCH)),
                dma((STEPS, natm - 1, FCH)),
                dma((STEPS, natm, FCH, 3)),
                dma((STEPS, natm, FCH, 3)),
            ],
            compiler_params=pltpu.CompilerParams(
                collective_id=0, has_side_effects=True, vmem_limit_bytes=66 * 1000 * 1000
            ),
        )(
            state,
            send_list,
            op_index.transpose(2, 0, 1),
            op_weight.reshape(nb, nk * bs, bs),
            vertical,
            flux_weight,
            remap_index.T,
            remap_weight.reshape(nb, nr * bs, bs),
            wet_mask.reshape(nb, bs),
        )

    in_specs = (
        P("sec", None, "dom"),
        P("sec", "dom", None, None),
        P("sec", "dom", None),
        P("sec", "dom", None, None, None),
        P("sec", None, None),
        P("sec", None, None),
        P("dom", None),
        P("dom", None, None, None),
        P("dom"),
    )
    return jax.shard_map(
        local, mesh=mesh, in_specs=in_specs, out_specs=P("sec", None, "dom"), check_vma=False
    )
```
